512 devices in a mesh: tm: 16 (over y_hi, x, core), space: 32 (over z, y_lo).
Axes of the slice: x: 4, y: 4 (y_hi: 2, y_lo: 2; y = y_hi * 2 + y_lo), z: 16, core: 2. Of those that a mesh axis runs over, the one named last changes fastest.
Arguments:
- start_states: float32 [16, 512, 1024], P('tm', 'space'), may hold values from -6 to 6
- sigma: float32 [512, 1024], P('space'), may hold values from 0.05 to 5
- labels: int32 [512, 1024], P('space'), may hold values from 0 to 3
- nu_table: float32 [4], replicated, may hold values from 0.3 to 3
- coil: float32 [512, 1024], P('space'), may hold values from -6 to 6
- waveform: float32 [256], P('tm'), may hold values from -4 to 4
Outputs:
- end_states: float32 [16, 512, 1024], P('tm', 'space')
- traces_out: float32 [256, 32768], P('tm', 'space')
The draws below stay inside these ranges and needn't reach their ends.
All inputs are finite; a program needn't handle non-finite values.
Results may differ from the reference program's by a relative error of at most 0.000026.
Values sent between devices are 32-bit elements; how exact they have to be, the bound alone decides.
A program may use at most 64 MiB of HBM per device.

```python
import math
import jax
import jax.numpy as jnp
from jax import lax

CX = 16
NY = 1024
STEPS = 16
JACOBI = 8
SWEEPS = 2
MATERIALS = 4
NX = 512
WINDOWS = 16
N_TM = 16
N_SPACE = 32


def touch_ends(values, stream_key, least, high):
    place = [jax.random.randint(jax.random.fold_in(stream_key, axis), (), 0, length) for axis, length in enumerate(values.shape)]
    longest = values.shape.index(max(values.shape))
    beside = place[:longest] + [(place[longest] + 1) % values.shape[longest]] + place[longest + 1:]
    return values.at[tuple(place)].set(least).at[tuple(beside)].set(high)


def block_scale(rng, dims, cuts, least, largest):
    factor_of = 1.0
    for position, blocks in cuts:
        steps = jax.random.uniform(jax.random.fold_in(jax.random.fold_in(rng, 6), position), (blocks,), jnp.float32, least / len(cuts), largest / len(cuts))
        factor_of = factor_of * jnp.repeat(jnp.exp(steps), dims[position] // blocks).reshape((-1,) + (1,) * (len(dims) - 1 - position))
    return factor_of


def normal_values(rng, shape, scale, bound, shards=(), kind=jnp.bfloat16):
    level = block_scale(rng, shape, shards, -0.22, 0.18) if shards else 1.0
    values = jax.random.normal(rng, shape, jnp.float32) * scale * level
    return jnp.minimum(jnp.maximum(values, -bound), bound).astype(kind)


def setup_inputs(seed: int = 0) -> dict:
    key_of = jax.random.split(jax.random.key(seed), 7)
    start_states = normal_values(key_of[0], (WINDOWS, NX, NY), 1.0, 6.0, ((0, 16), (1, 32)), jnp.float32)
    sigma = jnp.clip(jnp.exp(math.log(5.0) - 4.6051702 * jax.random.uniform(key_of[1], (NX, NY), jnp.float32) ** block_scale(key_of[1], (NX, NY), ((0, 32),), -0.2, 0.2)), 0.05, 5.0)
    labels = touch_ends(jax.random.randint(key_of[2], (NX, NY), 0, MATERIALS), jax.random.fold_in(key_of[2], 1), 0, MATERIALS - 1).astype(jnp.int32)
    nu_table = jnp.clip(jnp.exp(jax.random.uniform(key_of[3], (MATERIALS,), jnp.float32, math.log(0.3), math.log(3.0))), 0.3, 3.0)
    coil = normal_values(key_of[4], (NX, NY), 1.0, 6.0, ((0, 32),), jnp.float32)
    waveform = normal_values(key_of[5], (WINDOWS * STEPS,), 1.0, 4.0, ((0, 16),), jnp.float32)
    return {"start_states": start_states, "sigma": sigma, "labels": labels, "nu_table": nu_table, "coil": coil, "waveform": waveform}


THETA = 0.25


def shifted(field, axis, low, high):
    config = [(0, 0, 0)] * field.ndim
    config[axis % field.ndim] = (low, high, 0)
    return lax.pad(field, jnp.zeros((), field.dtype), config)


def next_column(field):
    return shifted(field, -2, -1, 1)


def prev_column(field):
    return shifted(field, -2, 1, -1)


def next_row(field):
    return shifted(field, -1, -1, 1)


def prev_row(field):
    return shifted(field, -1, 1, -1)


def from_next(array, axis):
    moved = jnp.moveaxis(array, axis, 0)
    moved = jnp.concatenate([moved[1:], jnp.zeros_like(moved[:1])], axis=0)
    return jnp.moveaxis(moved, 0, axis)


def from_prev(array, axis):
    moved = jnp.moveaxis(array, axis, 0)
    moved = jnp.concatenate([jnp.zeros_like(moved[:1]), moved[:-1]], axis=0)
    return jnp.moveaxis(moved, 0, axis)


def harmonic(first_nu, second_nu):
    return 2.0 * first_nu * second_nu / (first_nu + second_nu)


def reluctivity(labels, nu_table):
    result = jnp.zeros(labels.shape, jnp.float32)
    for material in range(nu_table.shape[0]):
        result = result + jnp.where(labels == material, nu_table[material], jnp.float32(0.0))
    return result


def coefficients(sigma, nu, first, last):
    kxp = harmonic(nu, next_column(nu))
    kxm = harmonic(nu, prev_column(nu))
    kyp = harmonic(nu, next_row(nu))
    kym = harmonic(nu, prev_row(nu))
    rows = jnp.arange(nu.shape[-1])
    edge_rows = ((rows == 0) | (rows == nu.shape[-1] - 1)).astype(jnp.float32)
    inner = sigma + kxp + kxm + kyp + kym + 2.0 * nu * edge_rows
    left_coef = 2.0 * nu[..., 0, :]
    right_coef = 2.0 * nu[..., -1, :]
    cols = jnp.arange(nu.shape[-2])[:, None]
    at_left = (cols == 0).astype(jnp.float32)
    at_right = (cols == nu.shape[-2] - 1).astype(jnp.float32)
    d_dir = inner + at_left * left_coef[..., None, :] + at_right * right_coef[..., None, :]
    d_neu = inner + at_left * (first * left_coef)[..., None, :] + at_right * (last * right_coef)[..., None, :]
    return (sigma, kxp, kxm, kyp, kym), left_coef, right_coef, d_dir, d_neu


def march(start, couple, diag, coil, waves, left_term, right_term):
    sigma, kxp, kxm, kyp, kym = couple
    cols = jnp.arange(start.shape[-2])[:, None]
    at_left = (cols == 0).astype(jnp.float32)
    at_right = (cols == start.shape[-2] - 1).astype(jnp.float32)

    def advance(previous, inputs):
        wave, left_val, right_val = inputs
        rhs = sigma * previous + coil * wave + at_left * left_val[..., None, :] + at_right * right_val[..., None, :]
        field = previous
        for repeat in range(JACOBI):
            total = rhs + kxp * next_column(field) + kxm * prev_column(field) + kyp * next_row(field) + kym * prev_row(field)
            field = total / diag
        return field, (field[..., 0, :], field[..., -1, :])

    return lax.scan(advance, start, (waves, left_term, right_term))


def reference(start_states, sigma, labels, nu_table, coil, waveform):
    nu = reluctivity(labels, nu_table).reshape(N_SPACE, CX, NY)
    sig = sigma.reshape(N_SPACE, CX, NY)
    coil_blocks = coil.reshape(N_SPACE, CX, NY)
    places = jnp.arange(N_SPACE)
    first = (places == 0).astype(jnp.float32)[:, None]
    last = (places == N_SPACE - 1).astype(jnp.float32)[:, None]
    couple, left_coef, right_coef, d_dir, d_neu = coefficients(sig, nu, first, last)
    waves = waveform.reshape(N_TM, STEPS).T.reshape(STEPS, N_TM, 1, 1, 1)
    zero_waves = jnp.zeros_like(waves)
    states = start_states.reshape(N_TM, N_SPACE, CX, NY)
    traces = jnp.zeros((STEPS, N_TM, N_SPACE, NY), jnp.float32)
    inner_face = 1.0 - last
    ends = states
    for relax_round in range(SWEEPS):
        left_val = from_prev(traces, 2)
        left_term = left_coef * left_val
        right_term = right_coef * traces
        ends, (firsts, lasts) = march(states, couple, d_dir, coil_blocks, waves, left_term, right_term)
        nb_first = from_next(firsts, 2)
        nb_coef = from_next(left_coef, 0)
        flux = inner_face * (right_coef * (lasts - traces) + nb_coef * (nb_first - traces))
        flux_left = from_prev(flux, 2)
        unused, (pfirst, plast) = march(jnp.zeros_like(states), couple, d_neu, coil_blocks, zero_waves, flux_left, flux)
        traces = traces + THETA * inner_face * (plast + from_next(pfirst, 2))
        if relax_round + 1 < SWEEPS:
            states = jnp.roll(ends, 1, axis=0)
    end_states = ends.reshape(N_TM, N_SPACE * CX, NY)
    traces_out = jnp.transpose(traces, (1, 0, 2, 3)).reshape(N_TM * STEPS, N_SPACE * NY)
    return end_states, traces_out
```

```python
import functools

import jax
import jax.numpy as jnp
from jax import lax
from jax.experimental import pallas as pl
from jax.experimental.pallas import tpu as pltpu
from jax.sharding import PartitionSpec as P

JACOBI = 8
SWEEPS = 2


THETA = 0.25


def passed_along(array, axis, by):
    peers = lax.axis_size(axis)
    pairs = [(i, i + by) for i in range(peers) if 0 <= i + by < peers]
    return lax.ppermute(array, axis, pairs)


def from_behind(value, axis, steps):
    count = lax.axis_size(axis)
    pairs = [(source, (source + steps) % count) for source in range(count)]
    return lax.ppermute(value, axis, pairs)


def shifted(field, axis, low, high):
    config = [(0, 0, 0)] * field.ndim
    config[axis % field.ndim] = (low, high, 0)
    return lax.pad(field, jnp.zeros((), field.dtype), config)


def next_column(field):
    return shifted(field, -2, -1, 1)


def prev_column(field):
    return shifted(field, -2, 1, -1)


def next_row(field):
    return shifted(field, -1, -1, 1)


def prev_row(field):
    return shifted(field, -1, 1, -1)


def harmonic(first_nu, second_nu):
    return 2.0 * first_nu * second_nu / (first_nu + second_nu)


def reluctivity(labels, nu_table):
    result = jnp.zeros(labels.shape, jnp.float32)
    for material in range(nu_table.shape[0]):
        result = result + jnp.where(labels == material, nu_table[material], jnp.float32(0.0))
    return result


def coefficients(sigma, nu, first, last):
    kxp = harmonic(nu, next_column(nu))
    kxm = harmonic(nu, prev_column(nu))
    kyp = harmonic(nu, next_row(nu))
    kym = harmonic(nu, prev_row(nu))
    rows = jnp.arange(nu.shape[-1])
    edge_rows = ((rows == 0) | (rows == nu.shape[-1] - 1)).astype(jnp.float32)
    inner = sigma + kxp + kxm + kyp + kym + 2.0 * nu * edge_rows
    left_coef = 2.0 * nu[..., 0, :]
    right_coef = 2.0 * nu[..., -1, :]
    cols = jnp.arange(nu.shape[-2])[:, None]
    at_left = (cols == 0).astype(jnp.float32)
    at_right = (cols == nu.shape[-2] - 1).astype(jnp.float32)
    d_dir = inner + at_left * left_coef[..., None, :] + at_right * right_coef[..., None, :]
    d_neu = (
        inner
        + at_left * (first * left_coef)[..., None, :]
        + at_right * (last * right_coef)[..., None, :]
    )
    return ((sigma, kxp, kxm, kyp, kym), left_coef, right_coef, d_dir, d_neu)


def march_kernel(forced, waves, start, sigma, coil, diag, axp, axm, ayp, aym,
                 left_term, right_term, end, firsts, lasts):
    cols_n, rows_n = start.shape
    cols = lax.broadcasted_iota(jnp.int32, (cols_n, rows_n), 0)

    def advance(step, previous):
        rhs = sigma[...] * previous
        if forced:
            rhs = rhs + coil[...] * waves[step]
        left_val = left_term[pl.ds(step, 1), :]
        right_val = right_term[pl.ds(step, 1), :]
        rhs = rhs + jnp.where(cols == 0, left_val, 0.0)
        rhs = rhs + jnp.where(cols == cols_n - 1, right_val, 0.0)
        base = rhs / diag[...]
        field = previous
        for repeat in range(JACOBI):
            field = (
                base
                + axp[...] * pltpu.roll(field, cols_n - 1, 0)
                + axm[...] * pltpu.roll(field, 1, 0)
                + ayp[...] * pltpu.roll(field, rows_n - 1, 1)
                + aym[...] * pltpu.roll(field, 1, 1)
            )
        firsts[pl.ds(step, 1), :] = field[0:1, :]
        lasts[pl.ds(step, 1), :] = field[cols_n - 1:cols_n, :]
        return field

    end[...] = lax.fori_loop(0, left_term.shape[0], advance, start[...])


def march(start, sigma, coil, diag, scaled, waves, left_term, right_term, forced):
    cols_n, rows_n = start.shape
    steps = left_term.shape[0]
    vmem = pl.BlockSpec(memory_space=pltpu.VMEM)
    field = jax.ShapeDtypeStruct((cols_n, rows_n), jnp.float32)
    series = jax.ShapeDtypeStruct((steps, rows_n), jnp.float32)
    return pl.pallas_call(
        functools.partial(march_kernel, forced),
        out_shape=(field, series, series),
        in_specs=[pl.BlockSpec(memory_space=pltpu.SMEM)] + [vmem] * 10,
        out_specs=(vmem, vmem, vmem),
    )(waves, start, sigma, coil, diag, *scaled, left_term, right_term)


def body(start_states, sigma, labels, nu_table, coil, waveform):
    states = start_states[0]
    nu = reluctivity(labels, nu_table)
    place = lax.axis_index("space")
    count = lax.axis_size("space")
    first = (place == 0).astype(jnp.float32)
    last = (place == count - 1).astype(jnp.float32)
    couple, left_coef, right_coef, d_dir, d_neu = coefficients(sigma, nu, first, last)
    ks = couple[1:]
    scaled_dir = tuple(k / d_dir for k in ks)
    scaled_neu = tuple(k / d_neu for k in ks)
    zero_waves = jnp.zeros_like(waveform)
    traces = jnp.zeros((waveform.shape[0], states.shape[1]), jnp.float32)
    left_traces = jnp.zeros_like(traces)
    inner_face = 1.0 - last
    ends = states
    zeros = jnp.zeros_like(states)
    for relax_round in range(SWEEPS):
        if relax_round > 0:
            left_traces = passed_along(traces, "space", 1)
        left_term = left_coef * left_traces
        right_term = right_coef * traces
        ends, firsts, lasts = march(
            states, sigma, coil, d_dir, scaled_dir, waveform, left_term, right_term, True
        )
        nb_first, nb_coef = passed_along((firsts, left_coef), "space", -1)
        flux = inner_face * (right_coef * (lasts - traces) + nb_coef * (nb_first - traces))
        flux_left = passed_along(flux, "space", 1)
        unused, pfirst, plast = march(
            zeros, sigma, coil, d_neu, scaled_neu, zero_waves, flux_left, flux, False
        )
        nb_pfirst = passed_along(pfirst, "space", -1)
        traces = traces + THETA * inner_face * (plast + nb_pfirst)
        if relax_round + 1 < SWEEPS:
            states = from_behind(ends, "tm", 1)
    return (ends[None], traces)


def solution(mesh):
    placed = (
        P("tm", "space", None),
        P("space", None),
        P("space", None),
        P(),
        P("space", None),
        P("tm"),
    )
    return jax.shard_map(
        body,
        mesh=mesh,
        in_specs=placed,
        out_specs=(P("tm", "space", None), P("tm", "space")),
        check_vma=False,
    )
```

```python
import functools

import jax
import jax.numpy as jnp
from jax import lax
from jax.experimental import pallas as pl
from jax.experimental.pallas import tpu as pltpu
from jax.sharding import PartitionSpec as P

JACOBI = 8
SWEEPS = 2


THETA = 0.25


def passed_along(array, axis, by):
    peers = lax.axis_size(axis)
    pairs = [(i, i + by) for i in range(peers) if 0 <= i + by < peers]
    return lax.ppermute(array, axis, pairs)


def from_behind(value, axis, steps):
    count = lax.axis_size(axis)
    pairs = [(source, (source + steps) % count) for source in range(count)]
    return lax.ppermute(value, axis, pairs)


def shifted(field, axis, low, high):
    config = [(0, 0, 0)] * field.ndim
    config[axis % field.ndim] = (low, high, 0)
    return lax.pad(field, jnp.zeros((), field.dtype), config)


def next_column(field):
    return shifted(field, -2, -1, 1)


def prev_column(field):
    return shifted(field, -2, 1, -1)


def next_row(field):
    return shifted(field, -1, -1, 1)


def prev_row(field):
    return shifted(field, -1, 1, -1)


def harmonic(first_nu, second_nu):
    return 2.0 * first_nu * second_nu / (first_nu + second_nu)


def reluctivity(labels, nu_table):
    result = jnp.zeros(labels.shape, jnp.float32)
    for material in range(nu_table.shape[0]):
        result = result + jnp.where(labels == material, nu_table[material], jnp.float32(0.0))
    return result


def coefficients(sigma, nu, first, last):
    kxp = harmonic(nu, next_column(nu))
    kxm = harmonic(nu, prev_column(nu))
    kyp = harmonic(nu, next_row(nu))
    kym = harmonic(nu, prev_row(nu))
    rows = jnp.arange(nu.shape[-1])
    edge_rows = ((rows == 0) | (rows == nu.shape[-1] - 1)).astype(jnp.float32)
    inner = sigma + kxp + kxm + kyp + kym + 2.0 * nu * edge_rows
    left_coef = 2.0 * nu[..., 0, :]
    right_coef = 2.0 * nu[..., -1, :]
    cols = jnp.arange(nu.shape[-2])[:, None]
    at_left = (cols == 0).astype(jnp.float32)
    at_right = (cols == nu.shape[-2] - 1).astype(jnp.float32)
    d_dir = inner + at_left * left_coef[..., None, :] + at_right * right_coef[..., None, :]
    d_neu = (
        inner
        + at_left * (first * left_coef)[..., None, :]
        + at_right * (last * right_coef)[..., None, :]
    )
    return ((sigma, kxp, kxm, kyp, kym), left_coef, right_coef, d_dir, d_neu)


MESH = pl.DeviceIdType.MESH


def march_steps(waves, sigma, coil, diag, scaled, start, left_term, right_term,
                end, firsts, lasts, forced):
    cols_n, rows_n = start.shape
    cols = lax.broadcasted_iota(jnp.int32, (cols_n, rows_n), 0)
    axp, axm, ayp, aym = scaled

    def advance(step, previous):
        rhs = sigma[...] * previous
        if forced:
            rhs = rhs + coil[...] * waves[step]
        left_val = left_term[pl.ds(step, 1), :]
        right_val = right_term[pl.ds(step, 1), :]
        rhs = rhs + jnp.where(cols == 0, left_val, 0.0)
        rhs = rhs + jnp.where(cols == cols_n - 1, right_val, 0.0)
        base = rhs / diag[...]
        field = previous
        for repeat in range(JACOBI):
            field = (
                base
                + axp[...] * pltpu.roll(field, cols_n - 1, 0)
                + axm[...] * pltpu.roll(field, 1, 0)
                + ayp[...] * pltpu.roll(field, rows_n - 1, 1)
                + aym[...] * pltpu.roll(field, 1, 1)
            )
        firsts[pl.ds(step, 1), :] = field[0:1, :]
        lasts[pl.ds(step, 1), :] = field[cols_n - 1:cols_n, :]
        return field

    end[...] = lax.fori_loop(0, left_term.shape[0], advance, start)


def relax_kernel(waves, states, sigma, coil, nu, d_dir, d_neu,
                 axp_d, axm_d, ayp_d, aym_d, axp_n, axm_n, ayp_n, aym_n,
                 ends, traces,
                 sent_first, lasts, flux, pfirst, plast, ends0, left_term, right_term,
                 got_first, flux_left, got_pfirst, left_traces, got_state,
                 send_sem, recv_sem):
    cols_n, rows_n = states.shape
    steps = traces.shape[0]
    n_space = lax.axis_size("space")
    n_tm = lax.axis_size("tm")
    me_s = lax.axis_index("space")
    me_t = lax.axis_index("tm")
    has_left = me_s > 0
    has_right = me_s < n_space - 1
    left = (me_t, lax.rem(me_s + n_space - 1, n_space))
    right = (me_t, lax.rem(me_s + 1, n_space))
    tm_next = (lax.rem(me_t + 1, n_tm), me_s)
    tm_prev = (lax.rem(me_t + n_tm - 1, n_tm), me_s)

    barrier = pltpu.get_barrier_semaphore()

    @pl.when(has_left)
    def _():
        pl.semaphore_signal(barrier, inc=1, device_id=left, device_id_type=MESH)

    @pl.when(has_right)
    def _():
        pl.semaphore_signal(barrier, inc=1, device_id=right, device_id_type=MESH)

    pl.semaphore_signal(barrier, inc=1, device_id=tm_next, device_id_type=MESH)
    pl.semaphore_signal(barrier, inc=1, device_id=tm_prev, device_id_type=MESH)
    pl.semaphore_wait(barrier, 2 + has_left.astype(jnp.int32) + has_right.astype(jnp.int32))

    left_coef = 2.0 * nu[0:1, :]
    right_coef = 2.0 * nu[cols_n - 1:cols_n, :]
    inner_face = jnp.where(has_right, 1.0, 0.0).astype(jnp.float32)

    def send(slot, src, dst, target, sends):
        copy = pltpu.make_async_remote_copy(
            src_ref=src, dst_ref=dst, send_sem=send_sem.at[slot],
            recv_sem=recv_sem.at[slot], device_id=target, device_id_type=MESH,
        )

        @pl.when(sends)
        def _():
            copy.start()

        return copy

    def finish(copy, sends, receives, dst):
        @pl.when(sends)
        def _():
            copy.wait_send()

        @pl.when(receives)
        def _():
            copy.wait_recv()

        @pl.when(jnp.logical_not(receives))
        def _():
            dst[...] = jnp.zeros(dst.shape, dst.dtype)

    traces[...] = jnp.zeros(traces.shape, jnp.float32)
    start = states[...]
    scaled_dir = (axp_d, axm_d, ayp_d, aym_d)
    scaled_neu = (axp_n, axm_n, ayp_n, aym_n)
    state_copy = None
    for sweep in range(SWEEPS):
        base = 5 * sweep
        if sweep > 0:
            copy = send(base + 0, traces, left_traces.at[sweep], right, has_right)
            finish(copy, has_right, has_left, left_traces.at[sweep])
            left_term[...] = left_coef * left_traces[sweep]
            state_copy.wait_send()
            state_copy.wait_recv()
            start = got_state[...]
        else:
            left_term[...] = jnp.zeros(left_term.shape, jnp.float32)
        right_term[...] = right_coef * traces[...]
        end = ends if sweep + 1 == SWEEPS else ends0
        march_steps(waves, sigma, coil, d_dir, scaled_dir, start, left_term, right_term,
                    end, sent_first.at[sweep, pl.ds(0, steps)], lasts, True)
        if sweep + 1 < SWEEPS:
            state_copy = send(base + 4, ends0, got_state, tm_next, True)
        sent_first[sweep, pl.ds(steps, 8), :] = jnp.broadcast_to(left_coef, (8, rows_n))
        copy = send(base + 1, sent_first.at[sweep], got_first.at[sweep], left, has_left)
        finish(copy, has_left, has_right, got_first.at[sweep])
        nb_first = got_first[sweep, pl.ds(0, steps), :]
        nb_coef = got_first[sweep, pl.ds(steps, 1), :]
        g = traces[...]
        flux[sweep] = inner_face * (right_coef * (lasts[...] - g) + nb_coef * (nb_first - g))
        copy = send(base + 2, flux.at[sweep], flux_left.at[sweep], right, has_right)
        finish(copy, has_right, has_left, flux_left.at[sweep])
        march_steps(waves, sigma, coil, d_neu, scaled_neu,
                    jnp.zeros((cols_n, rows_n), jnp.float32),
                    flux_left.at[sweep], flux.at[sweep],
                    ends0 if sweep + 1 == SWEEPS else left_term,
                    pfirst.at[sweep], plast, False)
        copy = send(base + 3, pfirst.at[sweep], got_pfirst.at[sweep], left, has_left)
        finish(copy, has_left, has_right, got_pfirst.at[sweep])
        traces[...] = traces[...] + THETA * inner_face * (plast[...] + got_pfirst[sweep])


def relax(waveform, states, sigma, coil, nu, d_dir, d_neu, scaled_dir, scaled_neu):
    cols_n, rows_n = states.shape
    steps = waveform.shape[0]
    vmem = pl.BlockSpec(memory_space=pltpu.VMEM)
    field = jax.ShapeDtypeStruct((cols_n, rows_n), jnp.float32)
    series = jax.ShapeDtypeStruct((steps, rows_n), jnp.float32)
    plane = pltpu.VMEM((steps, rows_n), jnp.float32)
    pair = pltpu.VMEM((SWEEPS, steps, rows_n), jnp.float32)
    return pl.pallas_call(
        relax_kernel,
        out_shape=(field, series),
        in_specs=[pl.BlockSpec(memory_space=pltpu.SMEM)] + [vmem] * 14,
        out_specs=(vmem, vmem),
        scratch_shapes=[
            pltpu.VMEM((SWEEPS, steps + 8, rows_n), jnp.float32),
            plane,
            pair,
            pair,
            plane,
            pltpu.VMEM((cols_n, rows_n), jnp.float32),
            pltpu.VMEM((cols_n, rows_n), jnp.float32),
            plane,
            pltpu.VMEM((SWEEPS, steps + 8, rows_n), jnp.float32),
            pair,
            pair,
            pair,
            pltpu.VMEM((cols_n, rows_n), jnp.float32),
            pltpu.SemaphoreType.DMA((5 * SWEEPS,)),
            pltpu.SemaphoreType.DMA((5 * SWEEPS,)),
        ],
        compiler_params=pltpu.CompilerParams(collective_id=0, has_side_effects=True),
    )(waveform, states, sigma, coil, nu, d_dir, d_neu, *scaled_dir, *scaled_neu)


def body(start_states, sigma, labels, nu_table, coil, waveform):
    states = start_states[0]
    nu = reluctivity(labels, nu_table)
    place = lax.axis_index("space")
    count = lax.axis_size("space")
    first = (place == 0).astype(jnp.float32)
    last = (place == count - 1).astype(jnp.float32)
    couple, left_coef, right_coef, d_dir, d_neu = coefficients(sigma, nu, first, last)
    ks = couple[1:]
    scaled_dir = tuple(k / d_dir for k in ks)
    scaled_neu = tuple(k / d_neu for k in ks)
    ends, traces = relax(waveform, states, sigma, coil, nu, d_dir, d_neu, scaled_dir, scaled_neu)
    return (ends[None], traces)


def solution(mesh):
    placed = (
        P("tm", "space", None),
        P("space", None),
        P("space", None),
        P(),
        P("space", None),
        P("tm"),
    )
    return jax.shard_map(
        body,
        mesh=mesh,
        in_specs=placed,
        out_specs=(P("tm", "space", None), P("tm", "space")),
        check_vma=False,
    )
```

```python
import functools

import jax
import jax.numpy as jnp
from jax import lax
from jax.experimental import pallas as pl
from jax.experimental.pallas import tpu as pltpu
from jax.sharding import PartitionSpec as P

JACOBI = 8
SWEEPS = 2


THETA = 0.25


def passed_along(array, axis, by):
    peers = lax.axis_size(axis)
    pairs = [(i, i + by) for i in range(peers) if 0 <= i + by < peers]
    return lax.ppermute(array, axis, pairs)


def from_behind(value, axis, steps):
    count = lax.axis_size(axis)
    pairs = [(source, (source + steps) % count) for source in range(count)]
    return lax.ppermute(value, axis, pairs)


def shifted(field, axis, low, high):
    config = [(0, 0, 0)] * field.ndim
    config[axis % field.ndim] = (low, high, 0)
    return lax.pad(field, jnp.zeros((), field.dtype), config)


def next_column(field):
    return shifted(field, -2, -1, 1)


def prev_column(field):
    return shifted(field, -2, 1, -1)


def next_row(field):
    return shifted(field, -1, -1, 1)


def prev_row(field):
    return shifted(field, -1, 1, -1)


def harmonic(first_nu, second_nu):
    return 2.0 * first_nu * second_nu / (first_nu + second_nu)


def reluctivity(labels, nu_table):
    result = jnp.zeros(labels.shape, jnp.float32)
    for material in range(nu_table.shape[0]):
        result = result + jnp.where(labels == material, nu_table[material], jnp.float32(0.0))
    return result


def coefficients(sigma, nu, first, last):
    kxp = harmonic(nu, next_column(nu))
    kxm = harmonic(nu, prev_column(nu))
    kyp = harmonic(nu, next_row(nu))
    kym = harmonic(nu, prev_row(nu))
    rows = jnp.arange(nu.shape[-1])
    edge_rows = ((rows == 0) | (rows == nu.shape[-1] - 1)).astype(jnp.float32)
    inner = sigma + kxp + kxm + kyp + kym + 2.0 * nu * edge_rows
    left_coef = 2.0 * nu[..., 0, :]
    right_coef = 2.0 * nu[..., -1, :]
    cols = jnp.arange(nu.shape[-2])[:, None]
    at_left = (cols == 0).astype(jnp.float32)
    at_right = (cols == nu.shape[-2] - 1).astype(jnp.float32)
    d_dir = inner + at_left * left_coef[..., None, :] + at_right * right_coef[..., None, :]
    d_neu = (
        inner
        + at_left * (first * left_coef)[..., None, :]
        + at_right * (last * right_coef)[..., None, :]
    )
    return ((sigma, kxp, kxm, kyp, kym), left_coef, right_coef, d_dir, d_neu)


MESH = pl.DeviceIdType.MESH


def march_steps(waves, sigma, coil, diag, scaled, start, left_term, right_term,
                end, firsts, lasts, forced):
    cols_n, subs, lanes = start.shape
    lane = lax.broadcasted_iota(jnp.int32, (1, subs, lanes), 2)
    at_first = lane == 0
    at_last = lane == lanes - 1
    axp, axm, ayp, aym = scaled

    def advance(step, previous):
        rhs = sigma[...] * previous
        if forced:
            rhs = rhs + coil[...] * waves[step]
        left_val = left_term[pl.ds(step, 1)]
        right_val = right_term[pl.ds(step, 1)]
        rhs = jnp.concatenate(
            [rhs[0:1] + left_val, rhs[1:cols_n - 1], rhs[cols_n - 1:] + right_val], axis=0
        )
        base = rhs / diag[...]
        field = previous
        for repeat in range(JACOBI):
            up = pltpu.roll(field, lanes - 1, 2)
            up = jnp.where(at_last, pltpu.roll(up, subs - 1, 1), up)
            down = pltpu.roll(field, 1, 2)
            down = jnp.where(at_first, pltpu.roll(down, 1, 1), down)
            east = jnp.concatenate([field[1:], field[:1]], axis=0)
            west = jnp.concatenate([field[cols_n - 1:], field[:cols_n - 1]], axis=0)
            field = (
                base
                + axp[...] * east
                + axm[...] * west
                + ayp[...] * up
                + aym[...] * down
            )
        firsts[pl.ds(step, 1)] = field[0:1]
        lasts[pl.ds(step, 1)] = field[cols_n - 1:]
        return field

    end[...] = lax.fori_loop(0, left_term.shape[0], advance, start)


def relax_kernel(waves, states, sigma, coil, nu, d_dir, d_neu,
                 axp_d, axm_d, ayp_d, aym_d, axp_n, axm_n, ayp_n, aym_n,
                 ends, traces,
                 sent_first, lasts, flux, pfirst, plast, ends0, left_term, right_term,
                 got_first, flux_left, got_pfirst, left_traces, got_state,
                 send_sem, recv_sem):
    cols_n, subs, lanes = states.shape
    steps = traces.shape[0]
    n_space = lax.axis_size("space")
    n_tm = lax.axis_size("tm")
    me_s = lax.axis_index("space")
    me_t = lax.axis_index("tm")
    has_left = me_s > 0
    has_right = me_s < n_space - 1
    left = (me_t, lax.rem(me_s + n_space - 1, n_space))
    right = (me_t, lax.rem(me_s + 1, n_space))
    tm_next = (lax.rem(me_t + 1, n_tm), me_s)
    tm_prev = (lax.rem(me_t + n_tm - 1, n_tm), me_s)

    barrier = pltpu.get_barrier_semaphore()

    @pl.when(has_left)
    def _():
        pl.semaphore_signal(barrier, inc=1, device_id=left, device_id_type=MESH)

    @pl.when(has_right)
    def _():
        pl.semaphore_signal(barrier, inc=1, device_id=right, device_id_type=MESH)

    pl.semaphore_signal(barrier, inc=1, device_id=tm_next, device_id_type=MESH)
    pl.semaphore_signal(barrier, inc=1, device_id=tm_prev, device_id_type=MESH)
    pl.semaphore_wait(barrier, 2 + has_left.astype(jnp.int32) + has_right.astype(jnp.int32))

    left_coef = 2.0 * nu[0:1]
    right_coef = 2.0 * nu[cols_n - 1:]
    inner_face = jnp.where(has_right, 1.0, 0.0).astype(jnp.float32)

    def send(slot, src, dst, target, sends):
        copy = pltpu.make_async_remote_copy(
            src_ref=src, dst_ref=dst, send_sem=send_sem.at[slot],
            recv_sem=recv_sem.at[slot], device_id=target, device_id_type=MESH,
        )

        @pl.when(sends)
        def _():
            copy.start()

        return copy

    def finish(copy, sends, receives, dst):
        @pl.when(sends)
        def _():
            copy.wait_send()

        @pl.when(receives)
        def _():
            copy.wait_recv()

        @pl.when(jnp.logical_not(receives))
        def _():
            dst[...] = jnp.zeros(dst.shape, dst.dtype)

    traces[...] = jnp.zeros(traces.shape, jnp.float32)
    start = states[...]
    scaled_dir = (axp_d, axm_d, ayp_d, aym_d)
    scaled_neu = (axp_n, axm_n, ayp_n, aym_n)
    state_copy = None
    for sweep in range(SWEEPS):
        base = 5 * sweep
        if sweep > 0:
            copy = send(base + 0, traces, left_traces.at[sweep], right, has_right)
            finish(copy, has_right, has_left, left_traces.at[sweep])
            left_term[...] = left_coef * left_traces[sweep]
            state_copy.wait_send()
            state_copy.wait_recv()
            start = got_state[...]
        else:
            left_term[...] = jnp.zeros(left_term.shape, jnp.float32)
        right_term[...] = right_coef * traces[...]
        end = ends if sweep + 1 == SWEEPS else ends0
        march_steps(waves, sigma, coil, d_dir, scaled_dir, start, left_term, right_term,
                    end, sent_first.at[sweep, pl.ds(0, steps)], lasts, True)
        if sweep + 1 < SWEEPS:
            state_copy = send(base + 4, ends0, got_state, tm_next, True)
        sent_first[sweep, pl.ds(steps, 1)] = left_coef
        copy = send(base + 1, sent_first.at[sweep], got_first.at[sweep], left, has_left)
        finish(copy, has_left, has_right, got_first.at[sweep])
        nb_first = got_first[sweep, pl.ds(0, steps)]
        nb_coef = got_first[sweep, pl.ds(steps, 1)]
        g = traces[...]
        flux[sweep] = inner_face * (right_coef * (lasts[...] - g) + nb_coef * (nb_first - g))
        copy = send(base + 2, flux.at[sweep], flux_left.at[sweep], right, has_right)
        finish(copy, has_right, has_left, flux_left.at[sweep])
        march_steps(waves, sigma, coil, d_neu, scaled_neu,
                    jnp.zeros((cols_n, subs, lanes), jnp.float32),
                    flux_left.at[sweep], flux.at[sweep],
                    ends0 if sweep + 1 == SWEEPS else left_term,
                    pfirst.at[sweep], plast, False)
        copy = send(base + 3, pfirst.at[sweep], got_pfirst.at[sweep], left, has_left)
        finish(copy, has_left, has_right, got_pfirst.at[sweep])
        traces[...] = traces[...] + THETA * inner_face * (plast[...] + got_pfirst[sweep])


def relax(waveform, states, sigma, coil, nu, d_dir, d_neu, scaled_dir, scaled_neu):
    cols_n, subs, lanes = states.shape
    steps = waveform.shape[0]
    vmem = pl.BlockSpec(memory_space=pltpu.VMEM)
    field = jax.ShapeDtypeStruct((cols_n, subs, lanes), jnp.float32)
    series = jax.ShapeDtypeStruct((steps, subs, lanes), jnp.float32)
    plane = pltpu.VMEM((steps, subs, lanes), jnp.float32)
    pair = pltpu.VMEM((SWEEPS, steps, subs, lanes), jnp.float32)
    with_coef = pltpu.VMEM((SWEEPS, steps + 1, subs, lanes), jnp.float32)
    return pl.pallas_call(
        relax_kernel,
        out_shape=(field, series),
        in_specs=[pl.BlockSpec(memory_space=pltpu.SMEM)] + [vmem] * 14,
        out_specs=(vmem, vmem),
        scratch_shapes=[
            with_coef,
            plane,
            pair,
            pair,
            plane,
            pltpu.VMEM((cols_n, subs, lanes), jnp.float32),
            pltpu.VMEM((cols_n, subs, lanes), jnp.float32),
            plane,
            with_coef,
            pair,
            pair,
            pair,
            pltpu.VMEM((cols_n, subs, lanes), jnp.float32),
            pltpu.SemaphoreType.DMA((5 * SWEEPS,)),
            pltpu.SemaphoreType.DMA((5 * SWEEPS,)),
        ],
        compiler_params=pltpu.CompilerParams(collective_id=0, has_side_effects=True),
    )(waveform, states, sigma, coil, nu, d_dir, d_neu, *scaled_dir, *scaled_neu)


def body(start_states, sigma, labels, nu_table, coil, waveform):
    states = start_states[0]
    nu = reluctivity(labels, nu_table)
    place = lax.axis_index("space")
    count = lax.axis_size("space")
    first = (place == 0).astype(jnp.float32)
    last = (place == count - 1).astype(jnp.float32)
    couple, left_coef, right_coef, d_dir, d_neu = coefficients(sigma, nu, first, last)
    ks = couple[1:]
    scaled_dir = tuple(k / d_dir for k in ks)
    scaled_neu = tuple(k / d_neu for k in ks)
    cols_n, rows_n = states.shape
    lanes = 128
    tiled = lambda x: x.reshape(x.shape[0], rows_n // lanes, lanes)
    ends, traces = relax(
        waveform, tiled(states), tiled(sigma), tiled(coil), tiled(nu), tiled(d_dir), tiled(d_neu),
        tuple(map(tiled, scaled_dir)), tuple(map(tiled, scaled_neu)),
    )
    return (ends.reshape(1, cols_n, rows_n), traces.reshape(traces.shape[0], rows_n))


def solution(mesh):
    placed = (
        P("tm", "space", None),
        P("space", None),
        P("space", None),
        P(),
        P("space", None),
        P("tm"),
    )
    return jax.shard_map(
        body,
        mesh=mesh,
        in_specs=placed,
        out_specs=(P("tm", "space", None), P("tm", "space")),
        check_vma=False,
    )
```

```python
import jax
import jax.numpy as jnp
from jax import lax
from jax.experimental import pallas as pl
from jax.experimental.pallas import tpu as pltpu
from jax.sharding import PartitionSpec as P

JACOBI = 8
SWEEPS = 2
LANES = 128


THETA = 0.25
MESH = pl.DeviceIdType.MESH


def harmonic(first_nu, second_nu):
    return 2.0 * first_nu * second_nu / (first_nu + second_nu)


def row_neighbours(field, at_first, at_last):
    subs, lanes = field.shape[1], field.shape[2]
    up = pltpu.roll(field, lanes - 1, 2)
    up = jnp.where(at_last, pltpu.roll(up, subs - 1, 1), up)
    down = pltpu.roll(field, 1, 2)
    down = jnp.where(at_first, pltpu.roll(down, 1, 1), down)
    return up, down


def march_steps(waves, sigma, coil, diag, scaled, start, left_term, right_term,
                end, firsts, lasts, forced):
    cols_n, subs, lanes = start.shape
    lane = lax.broadcasted_iota(jnp.int32, (1, subs, lanes), 2)
    at_first = lane == 0
    at_last = lane == lanes - 1
    axp, axm, ayp, aym = scaled

    def advance(step, previous):
        rhs = sigma[...] * previous
        if forced:
            rhs = rhs + coil[...] * waves[step]
        left_val = left_term[pl.ds(step, 1)]
        right_val = right_term[pl.ds(step, 1)]
        rhs = jnp.concatenate(
            [rhs[0:1] + left_val, rhs[1:cols_n - 1], rhs[cols_n - 1:] + right_val], axis=0
        )
        base = rhs / diag[...]
        field = previous
        for repeat in range(JACOBI):
            up, down = row_neighbours(field, at_first, at_last)
            east = jnp.concatenate([field[1:], field[:1]], axis=0)
            west = jnp.concatenate([field[cols_n - 1:], field[:cols_n - 1]], axis=0)
            field = (
                base
                + axp[...] * east
                + axm[...] * west
                + ayp[...] * up
                + aym[...] * down
            )
        firsts[pl.ds(step, 1)] = field[0:1]
        lasts[pl.ds(step, 1)] = field[cols_n - 1:]
        return field

    end[...] = lax.fori_loop(0, left_term.shape[0], advance, start)


def relax_kernel(waves, table, packed, ends, traces,
                 coef, sent_first, sent_last, pfirst, plast, ends0, spare,
                 left_term, right_term, g_left, flux_left, flux_right,
                 got_first, got_last, got_pfirst, got_plast, got_state,
                 send_sem, recv_sem):
    _, cols_n, subs, lanes = packed.shape
    steps = traces.shape[0]
    n_space = lax.axis_size("space")
    n_tm = lax.axis_size("tm")
    me_s = lax.axis_index("space")
    me_t = lax.axis_index("tm")
    has_left = me_s > 0
    has_right = me_s < n_space - 1
    left = (me_t, lax.rem(me_s + n_space - 1, n_space))
    right = (me_t, lax.rem(me_s + 1, n_space))
    tm_next = (lax.rem(me_t + 1, n_tm), me_s)
    tm_prev = (lax.rem(me_t + n_tm - 1, n_tm), me_s)

    barrier = pltpu.get_barrier_semaphore()

    @pl.when(has_left)
    def _():
        pl.semaphore_signal(barrier, inc=1, device_id=left, device_id_type=MESH)

    @pl.when(has_right)
    def _():
        pl.semaphore_signal(barrier, inc=1, device_id=right, device_id_type=MESH)

    pl.semaphore_signal(barrier, inc=1, device_id=tm_next, device_id_type=MESH)
    pl.semaphore_signal(barrier, inc=1, device_id=tm_prev, device_id_type=MESH)
    pl.semaphore_wait(barrier, 2 + has_left.astype(jnp.int32) + has_right.astype(jnp.int32))

    sigma = packed.at[1]
    coil = packed.at[2]
    labels = packed[3]
    nu = jnp.zeros(labels.shape, jnp.float32)
    for material in range(table.shape[0]):
        nu = nu + jnp.where(labels == jnp.float32(material), table[material], jnp.float32(0.0))
    lane = lax.broadcasted_iota(jnp.int32, (1, subs, lanes), 2)
    row = lax.broadcasted_iota(jnp.int32, (1, subs, lanes), 1) * lanes + lane
    rows_n = subs * lanes
    up, down = row_neighbours(nu, lane == 0, lane == lanes - 1)
    up = jnp.where(row == rows_n - 1, 0.0, up)
    down = jnp.where(row == 0, 0.0, down)
    blank = jnp.zeros((1, subs, lanes), jnp.float32)
    east = jnp.concatenate([nu[1:], blank], axis=0)
    west = jnp.concatenate([blank, nu[:cols_n - 1]], axis=0)
    kxp = harmonic(nu, east)
    kxm = harmonic(nu, west)
    kyp = harmonic(nu, up)
    kym = harmonic(nu, down)
    edge_rows = jnp.where((row == 0) | (row == rows_n - 1), 1.0, 0.0).astype(jnp.float32)
    inner = sigma[...] + kxp + kxm + kyp + kym + 2.0 * nu * edge_rows
    left_coef = 2.0 * nu[0:1]
    right_coef = 2.0 * nu[cols_n - 1:]
    first_f = jnp.where(has_left, 0.0, 1.0).astype(jnp.float32)
    last_f = jnp.where(has_right, 0.0, 1.0).astype(jnp.float32)
    inner_face = 1.0 - last_f
    d_dir = jnp.concatenate(
        [inner[0:1] + left_coef, inner[1:cols_n - 1], inner[cols_n - 1:] + right_coef], axis=0
    )
    d_neu = jnp.concatenate(
        [inner[0:1] + first_f * left_coef, inner[1:cols_n - 1],
         inner[cols_n - 1:] + last_f * right_coef], axis=0
    )
    coef[0] = d_dir
    coef[1] = d_neu
    for index, k in enumerate((kxp, kxm, kyp, kym)):
        coef[2 + index] = k / d_dir
        coef[6 + index] = k / d_neu
    scaled_dir = tuple(coef.at[2 + index] for index in range(4))
    scaled_neu = tuple(coef.at[6 + index] for index in range(4))

    def send(slot, src, dst, target, sends):
        copy = pltpu.make_async_remote_copy(
            src_ref=src, dst_ref=dst, send_sem=send_sem.at[slot],
            recv_sem=recv_sem.at[slot], device_id=target, device_id_type=MESH,
        )

        @pl.when(sends)
        def _():
            copy.start()

        return copy

    def finish(copy, sends, receives, dst):
        @pl.when(sends)
        def _():
            copy.wait_send()

        @pl.when(receives)
        def _():
            copy.wait_recv()

        @pl.when(jnp.logical_not(receives))
        def _():
            dst[...] = jnp.zeros(dst.shape, dst.dtype)

    traces[...] = jnp.zeros(traces.shape, jnp.float32)
    g_left[...] = jnp.zeros(g_left.shape, jnp.float32)
    start = packed[0]
    state_copy = None
    for sweep in range(SWEEPS):
        base = 5 * sweep
        if sweep > 0:
            left_term[...] = left_coef * g_left[...]
            right_term[...] = right_coef * traces[...]
            state_copy.wait_send()
            state_copy.wait_recv()
            start = got_state[...]
        else:
            left_term[...] = jnp.zeros(left_term.shape, jnp.float32)
            right_term[...] = jnp.zeros(right_term.shape, jnp.float32)
        end = ends if sweep + 1 == SWEEPS else ends0
        march_steps(waves, sigma, coil, coef.at[0], scaled_dir, start, left_term, right_term,
                    end, sent_first.at[sweep, pl.ds(0, steps)],
                    sent_last.at[sweep, pl.ds(0, steps)], True)
        if sweep + 1 < SWEEPS:
            state_copy = send(base + 4, ends0, got_state, tm_next, True)
        sent_first[sweep, pl.ds(steps, 1)] = left_coef
        sent_last[sweep, pl.ds(steps, 1)] = right_coef
        to_left = send(base + 0, sent_first.at[sweep], got_first.at[sweep], left, has_left)
        to_right = send(base + 1, sent_last.at[sweep], got_last.at[sweep], right, has_right)
        finish(to_left, has_left, has_right, got_first.at[sweep])
        finish(to_right, has_right, has_left, got_last.at[sweep])
        g = traces[...]
        lasts = sent_last[sweep, pl.ds(0, steps)]
        nb_first = got_first[sweep, pl.ds(0, steps)]
        nb_coef = got_first[sweep, pl.ds(steps, 1)]
        flux_right[...] = inner_face * (right_coef * (lasts - g) + nb_coef * (nb_first - g))
        gl = g_left[...]
        firsts = sent_first[sweep, pl.ds(0, steps)]
        nb_last = got_last[sweep, pl.ds(0, steps)]
        nb_rcoef = got_last[sweep, pl.ds(steps, 1)]
        from_left = 1.0 * (nb_rcoef * (nb_last - gl) + left_coef * (firsts - gl))
        flux_left[...] = jnp.where(has_left, from_left, 0.0)
        march_steps(waves, sigma, coil, coef.at[1], scaled_neu,
                    jnp.zeros((cols_n, subs, lanes), jnp.float32),
                    flux_left, flux_right,
                    ends0 if sweep + 1 == SWEEPS else spare,
                    pfirst.at[sweep], plast.at[sweep], False)
        to_left = send(base + 2, pfirst.at[sweep], got_pfirst.at[sweep], left, has_left)
        to_right = send(base + 3, plast.at[sweep], got_plast.at[sweep], right, has_right)
        finish(to_left, has_left, has_right, got_pfirst.at[sweep])
        finish(to_right, has_right, has_left, got_plast.at[sweep])
        traces[...] = traces[...] + THETA * inner_face * (plast[sweep] + got_pfirst[sweep])
        gl = g_left[...] + THETA * 1.0 * (got_plast[sweep] + pfirst[sweep])
        g_left[...] = jnp.where(has_left, gl, 0.0)


def relax(waveform, nu_table, packed):
    _, cols_n, subs, lanes = packed.shape
    steps = waveform.shape[0]
    vmem = pl.BlockSpec(memory_space=pltpu.VMEM)
    smem = pl.BlockSpec(memory_space=pltpu.SMEM)
    field = jax.ShapeDtypeStruct((cols_n, subs, lanes), jnp.float32)
    series = jax.ShapeDtypeStruct((steps, subs, lanes), jnp.float32)
    plane = pltpu.VMEM((steps, subs, lanes), jnp.float32)
    whole = pltpu.VMEM((cols_n, subs, lanes), jnp.float32)
    pair = pltpu.VMEM((SWEEPS, steps, subs, lanes), jnp.float32)
    with_coef = pltpu.VMEM((SWEEPS, steps + 1, subs, lanes), jnp.float32)
    return pl.pallas_call(
        relax_kernel,
        out_shape=(field, series),
        in_specs=[smem, smem, vmem],
        out_specs=(vmem, vmem),
        scratch_shapes=[
            pltpu.VMEM((10, cols_n, subs, lanes), jnp.float32),
            with_coef,
            with_coef,
            pair,
            pair,
            whole,
            whole,
            plane,
            plane,
            plane,
            plane,
            plane,
            with_coef,
            with_coef,
            pair,
            pair,
            whole,
            pltpu.SemaphoreType.DMA((5 * SWEEPS,)),
            pltpu.SemaphoreType.DMA((5 * SWEEPS,)),
        ],
        compiler_params=pltpu.CompilerParams(collective_id=0, has_side_effects=True),
    )(waveform, nu_table, packed)


def body(start_states, sigma, labels, nu_table, coil, waveform):
    states = start_states[0]
    cols_n, rows_n = states.shape
    packed = jnp.stack([states, sigma, coil, labels.astype(jnp.float32)])
    packed = packed.reshape(4, cols_n, rows_n // LANES, LANES)
    ends, traces = relax(waveform, nu_table, packed)
    return (ends.reshape(1, cols_n, rows_n), traces.reshape(traces.shape[0], rows_n))


def solution(mesh):
    placed = (
        P("tm", "space", None),
        P("space", None),
        P("space", None),
        P(),
        P("space", None),
        P("tm"),
    )
    return jax.shard_map(
        body,
        mesh=mesh,
        in_specs=placed,
        out_specs=(P("tm", "space", None), P("tm", "space")),
        check_vma=False,
    )
```

```python
import jax
import jax.numpy as jnp
from jax import lax
from jax.experimental import pallas as pl
from jax.experimental.pallas import tpu as pltpu
from jax.sharding import PartitionSpec as P

JACOBI = 8
SWEEPS = 2
LANES = 128


THETA = 0.25
MESH = pl.DeviceIdType.MESH


def harmonic(first_nu, second_nu):
    return 2.0 * first_nu * second_nu / (first_nu + second_nu)


def row_neighbours(field, at_first, at_last):
    subs, lanes = field.shape[1], field.shape[2]
    up = pltpu.roll(field, lanes - 1, 2)
    up = jnp.where(at_last, pltpu.roll(up, subs - 1, 1), up)
    down = pltpu.roll(field, 1, 2)
    down = jnp.where(at_first, pltpu.roll(down, 1, 1), down)
    return up, down


def march_steps(waves, sigma, coil, diag, scaled, start, forced, terms, after, end):
    cols_n, subs, lanes = start.shape
    lane = lax.broadcasted_iota(jnp.int32, (subs, lanes), 1)
    at_first = lane == 0
    at_last = lane == lanes - 1
    axp, axm, ayp, aym = scaled

    def advance(step, previous):
        rhs = sigma[...] * jnp.stack(previous)
        if forced:
            rhs = rhs + coil[...] * waves[step]
        left_val, right_val = terms(step)
        rhs = jnp.concatenate(
            [rhs[0:1] + left_val, rhs[1:cols_n - 1], rhs[cols_n - 1:] + right_val], axis=0
        )
        base = rhs / diag[...]
        field = list(previous)
        for repeat in range(JACOBI):
            fresh = []
            for col in range(cols_n):
                here = field[col]
                up = pltpu.roll(here, lanes - 1, 1)
                up = jnp.where(at_last, pltpu.roll(up, subs - 1, 0), up)
                down = pltpu.roll(here, 1, 1)
                down = jnp.where(at_first, pltpu.roll(down, 1, 0), down)
                across = base[col]
                if col + 1 < cols_n:
                    across = across + axp[col] * field[col + 1]
                if col > 0:
                    across = across + axm[col] * field[col - 1]
                fresh.append(across + (ayp[col] * up + aym[col] * down))
            field = fresh
        after(step, field)
        return tuple(field)

    done = lax.fori_loop(0, waves.shape[0], advance,
                         tuple(start[col] for col in range(cols_n)))
    end[...] = jnp.stack(done)


def relax_kernel(waves, table, packed, ends, traces,
                 coef, sent_first, sent_last, pfirst, plast, ends0, spare, g_left,
                 own_coefs, got_coefs, got_first, got_last, got_pfirst, got_plast, got_state,
                 send_sem, recv_sem):
    _, cols_n, subs, lanes = packed.shape
    steps = traces.shape[0]
    n_space = lax.axis_size("space")
    n_tm = lax.axis_size("tm")
    me_s = lax.axis_index("space")
    me_t = lax.axis_index("tm")
    has_left = me_s > 0
    has_right = me_s < n_space - 1
    no_left = jnp.logical_not(has_left)
    no_right = jnp.logical_not(has_right)
    left = (me_t, lax.rem(me_s + n_space - 1, n_space))
    right = (me_t, lax.rem(me_s + 1, n_space))
    tm_next = (lax.rem(me_t + 1, n_tm), me_s)
    tm_prev = (lax.rem(me_t + n_tm - 1, n_tm), me_s)

    @pl.when(no_right)
    def _():
        got_first[...] = jnp.zeros(got_first.shape, jnp.float32)
        got_pfirst[...] = jnp.zeros(got_pfirst.shape, jnp.float32)
        got_coefs[0] = jnp.zeros(got_coefs.shape[1:], jnp.float32)

    @pl.when(no_left)
    def _():
        got_last[...] = jnp.zeros(got_last.shape, jnp.float32)
        got_plast[...] = jnp.zeros(got_plast.shape, jnp.float32)
        got_coefs[1] = jnp.zeros(got_coefs.shape[1:], jnp.float32)

    barrier = pltpu.get_barrier_semaphore()

    @pl.when(has_left)
    def _():
        pl.semaphore_signal(barrier, inc=1, device_id=left, device_id_type=MESH)

    @pl.when(has_right)
    def _():
        pl.semaphore_signal(barrier, inc=1, device_id=right, device_id_type=MESH)

    pl.semaphore_signal(barrier, inc=1, device_id=tm_next, device_id_type=MESH)
    pl.semaphore_signal(barrier, inc=1, device_id=tm_prev, device_id_type=MESH)
    pl.semaphore_wait(barrier, 2 + has_left.astype(jnp.int32) + has_right.astype(jnp.int32))

    def copy_of(slot, src, dst, target):
        return pltpu.make_async_remote_copy(
            src_ref=src, dst_ref=dst, send_sem=send_sem.at[slot],
            recv_sem=recv_sem.at[slot], device_id=target, device_id_type=MESH,
        )

    def start_if(copy, sends):
        @pl.when(sends)
        def _():
            copy.start()

    def wait_send_if(copy, sends):
        @pl.when(sends)
        def _():
            copy.wait_send()

    def wait_recv_if(copy, receives):
        @pl.when(receives)
        def _():
            copy.wait_recv()

    sigma = packed.at[1]
    coil = packed.at[2]
    labels = packed[3]
    nu = jnp.zeros(labels.shape, jnp.float32)
    for material in range(table.shape[0]):
        nu = nu + jnp.where(labels == jnp.float32(material), table[material], jnp.float32(0.0))
    left_coef = 2.0 * nu[0:1]
    right_coef = 2.0 * nu[cols_n - 1:]
    own_coefs[0] = left_coef[0]
    own_coefs[1] = right_coef[0]
    coef_left = copy_of(0, own_coefs.at[0], got_coefs.at[0], left)
    coef_right = copy_of(1, own_coefs.at[1], got_coefs.at[1], right)
    start_if(coef_left, has_left)
    start_if(coef_right, has_right)

    lane = lax.broadcasted_iota(jnp.int32, (1, subs, lanes), 2)
    row = lax.broadcasted_iota(jnp.int32, (1, subs, lanes), 1) * lanes + lane
    rows_n = subs * lanes
    up, down = row_neighbours(nu, lane == 0, lane == lanes - 1)
    up = jnp.where(row == rows_n - 1, 0.0, up)
    down = jnp.where(row == 0, 0.0, down)
    blank = jnp.zeros((1, subs, lanes), jnp.float32)
    east = jnp.concatenate([nu[1:], blank], axis=0)
    west = jnp.concatenate([blank, nu[:cols_n - 1]], axis=0)
    kxp = harmonic(nu, east)
    kxm = harmonic(nu, west)
    kyp = harmonic(nu, up)
    kym = harmonic(nu, down)
    edge_rows = jnp.where((row == 0) | (row == rows_n - 1), 1.0, 0.0).astype(jnp.float32)
    inner = sigma[...] + kxp + kxm + kyp + kym + 2.0 * nu * edge_rows
    first_f = jnp.where(has_left, 0.0, 1.0).astype(jnp.float32)
    last_f = jnp.where(has_right, 0.0, 1.0).astype(jnp.float32)
    inner_face = 1.0 - last_f
    d_dir = jnp.concatenate(
        [inner[0:1] + left_coef, inner[1:cols_n - 1], inner[cols_n - 1:] + right_coef], axis=0
    )
    d_neu = jnp.concatenate(
        [inner[0:1] + first_f * left_coef, inner[1:cols_n - 1],
         inner[cols_n - 1:] + last_f * right_coef], axis=0
    )
    coef[0] = d_dir
    coef[1] = d_neu
    for index, k in enumerate((kxp, kxm, kyp, kym)):
        coef[2 + index] = k / d_dir
        coef[6 + index] = k / d_neu
    scaled_dir = tuple(coef.at[2 + index] for index in range(4))
    scaled_neu = tuple(coef.at[6 + index] for index in range(4))

    wait_send_if(coef_left, has_left)
    wait_send_if(coef_right, has_right)
    wait_recv_if(coef_left, has_right)
    wait_recv_if(coef_right, has_left)
    nb_coef = got_coefs[0][None]
    nb_rcoef = got_coefs[1][None]

    def row_copies(slot, src, dst, sweep, step):
        to_left = copy_of(slot + step, src[0].at[sweep, pl.ds(step, 1)],
                          dst[0].at[sweep, pl.ds(step, 1)], left)
        to_right = copy_of(slot + steps + step, src[1].at[sweep, pl.ds(step, 1)],
                           dst[1].at[sweep, pl.ds(step, 1)], right)
        return to_left, to_right

    def send_rows(slot, src, dst, sweep, step):
        to_left, to_right = row_copies(slot, src, dst, sweep, step)
        start_if(to_left, has_left)
        start_if(to_right, has_right)

    def settle_rows(slot, src, dst, sweep, step):
        to_left, to_right = row_copies(slot, src, dst, sweep, step)
        wait_send_if(to_left, has_left)
        wait_send_if(to_right, has_right)
        wait_recv_if(to_left, has_right)
        wait_recv_if(to_right, has_left)

    def face_slot(sweep):
        return 3 + 8 * steps * sweep

    def trace_slot(sweep):
        return 3 + 8 * steps * sweep + 4 * steps

    faces = ((sent_first, sent_last), (got_first, got_last))
    neumann = ((pfirst, plast), (got_pfirst, got_plast))

    def update_traces(sweep, step):
        settle_rows(trace_slot(sweep), neumann[0], neumann[1], sweep, step)
        g = traces[pl.ds(step, 1)]
        g = g + THETA * inner_face * (plast[sweep, pl.ds(step, 1)] + got_pfirst[sweep, pl.ds(step, 1)])
        traces[pl.ds(step, 1)] = g
        gl = g_left[pl.ds(step, 1)]
        gl = gl + THETA * 1.0 * (got_plast[sweep, pl.ds(step, 1)] + pfirst[sweep, pl.ds(step, 1)])
        gl = jnp.where(has_left, gl, 0.0)
        g_left[pl.ds(step, 1)] = gl
        return g, gl

    def keeper(slot, rows, sweep):
        def after(step, field):
            rows[0][sweep, pl.ds(step, 1)] = field[0][None]
            rows[1][sweep, pl.ds(step, 1)] = field[cols_n - 1][None]

            @pl.when(step > 0)
            def _():
                send_rows(slot, rows, faces[1] if rows is faces[0] else neumann[1],
                          sweep, step - 1)

        return after

    traces[...] = jnp.zeros(traces.shape, jnp.float32)
    g_left[...] = jnp.zeros(g_left.shape, jnp.float32)
    start = packed[0]
    state_copy = copy_of(2, ends0, got_state, tm_next)
    for sweep in range(SWEEPS):
        if sweep > 0:
            state_copy.wait_send()
            state_copy.wait_recv()
            start = got_state[...]

            def dirichlet_terms(step, sweep=sweep):
                g, gl = update_traces(sweep - 1, step)
                return left_coef * gl, right_coef * g
        else:
            def dirichlet_terms(step):
                return blank, blank
        end = ends if sweep + 1 == SWEEPS else ends0
        march_steps(waves, sigma, coil, coef.at[0], scaled_dir, start, True, dirichlet_terms,
                    keeper(face_slot(sweep), faces[0], sweep), end)
        send_rows(face_slot(sweep), faces[0], faces[1], sweep, steps - 1)
        if sweep + 1 < SWEEPS:
            state_copy.start()

        def neumann_terms(step, sweep=sweep):
            settle_rows(face_slot(sweep), faces[0], faces[1], sweep, step)
            g = traces[pl.ds(step, 1)]
            lasts = sent_last[sweep, pl.ds(step, 1)]
            nb_first = got_first[sweep, pl.ds(step, 1)]
            flux_right = inner_face * (right_coef * (lasts - g) + nb_coef * (nb_first - g))
            gl = g_left[pl.ds(step, 1)]
            firsts = sent_first[sweep, pl.ds(step, 1)]
            nb_last = got_last[sweep, pl.ds(step, 1)]
            from_left = 1.0 * (nb_rcoef * (nb_last - gl) + left_coef * (firsts - gl))
            return jnp.where(has_left, from_left, 0.0), flux_right

        march_steps(waves, sigma, coil, coef.at[1], scaled_neu,
                    jnp.zeros((cols_n, subs, lanes), jnp.float32), False, neumann_terms,
                    keeper(trace_slot(sweep), neumann[0], sweep),
                    ends0 if sweep + 1 == SWEEPS else spare)
        send_rows(trace_slot(sweep), neumann[0], neumann[1], sweep, steps - 1)

    def last_update(step, carry):
        update_traces(SWEEPS - 1, step)
        return carry

    lax.fori_loop(0, steps, last_update, 0)


def relax(waveform, nu_table, packed):
    _, cols_n, subs, lanes = packed.shape
    steps = waveform.shape[0]
    vmem = pl.BlockSpec(memory_space=pltpu.VMEM)
    smem = pl.BlockSpec(memory_space=pltpu.SMEM)
    field = jax.ShapeDtypeStruct((cols_n, subs, lanes), jnp.float32)
    series = jax.ShapeDtypeStruct((steps, subs, lanes), jnp.float32)
    plane = pltpu.VMEM((steps, subs, lanes), jnp.float32)
    whole = pltpu.VMEM((cols_n, subs, lanes), jnp.float32)
    pair = pltpu.VMEM((SWEEPS, steps, subs, lanes), jnp.float32)
    two = pltpu.VMEM((2, subs, lanes), jnp.float32)
    return pl.pallas_call(
        relax_kernel,
        out_shape=(field, series),
        in_specs=[smem, smem, vmem],
        out_specs=(vmem, vmem),
        scratch_shapes=[
            pltpu.VMEM((10, cols_n, subs, lanes), jnp.float32),
            pair,
            pair,
            pair,
            pair,
            whole,
            whole,
            plane,
            two,
            two,
            pair,
            pair,
            pair,
            pair,
            whole,
            pltpu.SemaphoreType.DMA((3 + 8 * steps * SWEEPS,)),
            pltpu.SemaphoreType.DMA((3 + 8 * steps * SWEEPS,)),
        ],
        compiler_params=pltpu.CompilerParams(collective_id=0, has_side_effects=True),
    )(waveform, nu_table, packed)


def body(start_states, sigma, labels, nu_table, coil, waveform):
    states = start_states[0]
    cols_n, rows_n = states.shape
    packed = jnp.stack([states, sigma, coil, labels.astype(jnp.float32)])
    packed = packed.reshape(4, cols_n, rows_n // LANES, LANES)
    ends, traces = relax(waveform, nu_table, packed)
    return (ends.reshape(1, cols_n, rows_n), traces.reshape(traces.shape[0], rows_n))


def solution(mesh):
    placed = (
        P("tm", "space", None),
        P("space", None),
        P("space", None),
        P(),
        P("space", None),
        P("tm"),
    )
    return jax.shard_map(
        body,
        mesh=mesh,
        in_specs=placed,
        out_specs=(P("tm", "space", None), P("tm", "space")),
        check_vma=False,
    )
```

```python
import jax
import jax.numpy as jnp
from jax import lax
from jax.experimental import pallas as pl
from jax.experimental.pallas import tpu as pltpu
from jax.sharding import PartitionSpec as P

JACOBI = 8
SWEEPS = 2
LANES = 128


THETA = 0.25
MESH = pl.DeviceIdType.MESH


def harmonic(first_nu, second_nu):
    return 2.0 * first_nu * second_nu / (first_nu + second_nu)


def row_neighbours(field, sub):
    subs, lanes = field.shape[-2], field.shape[-1]
    ahead = pltpu.roll(field, subs - 1, field.ndim - 2)
    behind = pltpu.roll(field, 1, field.ndim - 2)
    edges = jnp.where(sub == 0, behind, ahead)
    edges = pltpu.roll(edges, 1, field.ndim - 1,
                       stride=(lanes - 2) // (subs - 1), stride_axis=field.ndim - 2)
    up = jnp.where(sub == subs - 1, edges, ahead)
    down = jnp.where(sub == 0, edges, behind)
    return up, down


def march_steps(waves, sigma, coil, diag, scaled, start, forced, terms, after, end):
    cols_n, subs, lanes = start.shape
    sub = lax.broadcasted_iota(jnp.int32, (subs, lanes), 0)
    axp, axm, ayp, aym = scaled

    def advance(step, previous):
        rhs = sigma[...] * jnp.stack(previous)
        if forced:
            rhs = rhs + coil[...] * waves[step]
        left_val, right_val = terms(step)
        rhs = jnp.concatenate(
            [rhs[0:1] + left_val, rhs[1:cols_n - 1], rhs[cols_n - 1:] + right_val], axis=0
        )
        base = rhs / diag[...]
        field = list(previous)
        for repeat in range(JACOBI):
            fresh = []
            for col in range(cols_n):
                here = field[col]
                up, down = row_neighbours(here, sub)
                across = base[col]
                if col + 1 < cols_n:
                    across = across + axp[col] * field[col + 1]
                if col > 0:
                    across = across + axm[col] * field[col - 1]
                fresh.append(across + (ayp[col] * up + aym[col] * down))
            field = fresh
        after(step, field)
        return tuple(field)

    done = lax.fori_loop(0, waves.shape[0], advance,
                         tuple(start[col] for col in range(cols_n)))
    end[...] = jnp.stack(done)


def relax_kernel(waves, table, packed, ends, traces,
                 coef, sent_first, sent_last, pfirst, plast, ends0, spare, g_left,
                 own_coefs, got_coefs, got_first, got_last, got_pfirst, got_plast, got_state,
                 send_sem, recv_sem):
    _, cols_n, subs, lanes = packed.shape
    steps = traces.shape[0]
    n_space = lax.axis_size("space")
    n_tm = lax.axis_size("tm")
    me_s = lax.axis_index("space")
    me_t = lax.axis_index("tm")
    has_left = me_s > 0
    has_right = me_s < n_space - 1
    no_left = jnp.logical_not(has_left)
    no_right = jnp.logical_not(has_right)
    left = (me_t, lax.rem(me_s + n_space - 1, n_space))
    right = (me_t, lax.rem(me_s + 1, n_space))
    tm_next = (lax.rem(me_t + 1, n_tm), me_s)
    tm_prev = (lax.rem(me_t + n_tm - 1, n_tm), me_s)

    @pl.when(no_right)
    def _():
        got_first[...] = jnp.zeros(got_first.shape, jnp.float32)
        got_pfirst[...] = jnp.zeros(got_pfirst.shape, jnp.float32)
        got_coefs[0] = jnp.zeros(got_coefs.shape[1:], jnp.float32)

    @pl.when(no_left)
    def _():
        got_last[...] = jnp.zeros(got_last.shape, jnp.float32)
        got_plast[...] = jnp.zeros(got_plast.shape, jnp.float32)
        got_coefs[1] = jnp.zeros(got_coefs.shape[1:], jnp.float32)

    barrier = pltpu.get_barrier_semaphore()

    @pl.when(has_left)
    def _():
        pl.semaphore_signal(barrier, inc=1, device_id=left, device_id_type=MESH)

    @pl.when(has_right)
    def _():
        pl.semaphore_signal(barrier, inc=1, device_id=right, device_id_type=MESH)

    pl.semaphore_signal(barrier, inc=1, device_id=tm_next, device_id_type=MESH)
    pl.semaphore_signal(barrier, inc=1, device_id=tm_prev, device_id_type=MESH)
    pl.semaphore_wait(barrier, 2 + has_left.astype(jnp.int32) + has_right.astype(jnp.int32))

    def copy_of(slot, src, dst, target):
        return pltpu.make_async_remote_copy(
            src_ref=src, dst_ref=dst, send_sem=send_sem.at[slot],
            recv_sem=recv_sem.at[slot], device_id=target, device_id_type=MESH,
        )

    def start_if(copy, sends):
        @pl.when(sends)
        def _():
            copy.start()

    def wait_send_if(copy, sends):
        @pl.when(sends)
        def _():
            copy.wait_send()

    def wait_recv_if(copy, receives):
        @pl.when(receives)
        def _():
            copy.wait_recv()

    sigma = packed.at[1]
    coil = packed.at[2]
    labels = packed[3]
    nu = jnp.zeros(labels.shape, jnp.float32)
    for material in range(table.shape[0]):
        nu = nu + jnp.where(labels == jnp.float32(material), table[material], jnp.float32(0.0))
    left_coef = 2.0 * nu[0:1]
    right_coef = 2.0 * nu[cols_n - 1:]
    own_coefs[0] = left_coef[0]
    own_coefs[1] = right_coef[0]
    coef_left = copy_of(0, own_coefs.at[0], got_coefs.at[0], left)
    coef_right = copy_of(1, own_coefs.at[1], got_coefs.at[1], right)
    start_if(coef_left, has_left)
    start_if(coef_right, has_right)

    sub = lax.broadcasted_iota(jnp.int32, (1, subs, lanes), 1)
    row = lax.broadcasted_iota(jnp.int32, (1, subs, lanes), 2) * subs + sub
    rows_n = subs * lanes
    up, down = row_neighbours(nu, sub)
    up = jnp.where(row == rows_n - 1, 0.0, up)
    down = jnp.where(row == 0, 0.0, down)
    blank = jnp.zeros((1, subs, lanes), jnp.float32)
    east = jnp.concatenate([nu[1:], blank], axis=0)
    west = jnp.concatenate([blank, nu[:cols_n - 1]], axis=0)
    kxp = harmonic(nu, east)
    kxm = harmonic(nu, west)
    kyp = harmonic(nu, up)
    kym = harmonic(nu, down)
    edge_rows = jnp.where((row == 0) | (row == rows_n - 1), 1.0, 0.0).astype(jnp.float32)
    inner = sigma[...] + kxp + kxm + kyp + kym + 2.0 * nu * edge_rows
    first_f = jnp.where(has_left, 0.0, 1.0).astype(jnp.float32)
    last_f = jnp.where(has_right, 0.0, 1.0).astype(jnp.float32)
    inner_face = 1.0 - last_f
    d_dir = jnp.concatenate(
        [inner[0:1] + left_coef, inner[1:cols_n - 1], inner[cols_n - 1:] + right_coef], axis=0
    )
    d_neu = jnp.concatenate(
        [inner[0:1] + first_f * left_coef, inner[1:cols_n - 1],
         inner[cols_n - 1:] + last_f * right_coef], axis=0
    )
    coef[0] = d_dir
    coef[1] = d_neu
    for index, k in enumerate((kxp, kxm, kyp, kym)):
        coef[2 + index] = k / d_dir
        coef[6 + index] = k / d_neu
    scaled_dir = tuple(coef.at[2 + index] for index in range(4))
    scaled_neu = tuple(coef.at[6 + index] for index in range(4))

    wait_send_if(coef_left, has_left)
    wait_send_if(coef_right, has_right)
    wait_recv_if(coef_left, has_right)
    wait_recv_if(coef_right, has_left)
    nb_coef = got_coefs[0][None]
    nb_rcoef = got_coefs[1][None]

    def row_copies(slot, src, dst, sweep, step):
        to_left = copy_of(slot + step, src[0].at[sweep, pl.ds(step, 1)],
                          dst[0].at[sweep, pl.ds(step, 1)], left)
        to_right = copy_of(slot + steps + step, src[1].at[sweep, pl.ds(step, 1)],
                           dst[1].at[sweep, pl.ds(step, 1)], right)
        return to_left, to_right

    def send_rows(slot, src, dst, sweep, step):
        to_left, to_right = row_copies(slot, src, dst, sweep, step)
        start_if(to_left, has_left)
        start_if(to_right, has_right)

    def settle_rows(slot, src, dst, sweep, step):
        to_left, to_right = row_copies(slot, src, dst, sweep, step)
        wait_send_if(to_left, has_left)
        wait_send_if(to_right, has_right)
        wait_recv_if(to_left, has_right)
        wait_recv_if(to_right, has_left)

    def face_slot(sweep):
        return 3 + 8 * steps * sweep

    def trace_slot(sweep):
        return 3 + 8 * steps * sweep + 4 * steps

    faces = ((sent_first, sent_last), (got_first, got_last))
    neumann = ((pfirst, plast), (got_pfirst, got_plast))

    def update_traces(sweep, step):
        settle_rows(trace_slot(sweep), neumann[0], neumann[1], sweep, step)
        g = traces[pl.ds(step, 1)]
        g = g + THETA * inner_face * (plast[sweep, pl.ds(step, 1)] + got_pfirst[sweep, pl.ds(step, 1)])
        traces[pl.ds(step, 1)] = g
        gl = g_left[pl.ds(step, 1)]
        gl = gl + THETA * 1.0 * (got_plast[sweep, pl.ds(step, 1)] + pfirst[sweep, pl.ds(step, 1)])
        gl = jnp.where(has_left, gl, 0.0)
        g_left[pl.ds(step, 1)] = gl
        return g, gl

    def keeper(slot, rows, sweep):
        def after(step, field):
            rows[0][sweep, pl.ds(step, 1)] = field[0][None]
            rows[1][sweep, pl.ds(step, 1)] = field[cols_n - 1][None]

            @pl.when(step > 0)
            def _():
                send_rows(slot, rows, faces[1] if rows is faces[0] else neumann[1],
                          sweep, step - 1)

        return after

    traces[...] = jnp.zeros(traces.shape, jnp.float32)
    g_left[...] = jnp.zeros(g_left.shape, jnp.float32)
    start = packed[0]
    state_copy = copy_of(2, ends0, got_state, tm_next)
    for sweep in range(SWEEPS):
        if sweep > 0:
            state_copy.wait_send()
            state_copy.wait_recv()
            start = got_state[...]

            def dirichlet_terms(step, sweep=sweep):
                g, gl = update_traces(sweep - 1, step)
                return left_coef * gl, right_coef * g
        else:
            def dirichlet_terms(step):
                return blank, blank
        end = ends if sweep + 1 == SWEEPS else ends0
        march_steps(waves, sigma, coil, coef.at[0], scaled_dir, start, True, dirichlet_terms,
                    keeper(face_slot(sweep), faces[0], sweep), end)
        send_rows(face_slot(sweep), faces[0], faces[1], sweep, steps - 1)
        if sweep + 1 < SWEEPS:
            state_copy.start()

        def neumann_terms(step, sweep=sweep):
            settle_rows(face_slot(sweep), faces[0], faces[1], sweep, step)
            g = traces[pl.ds(step, 1)]
            lasts = sent_last[sweep, pl.ds(step, 1)]
            nb_first = got_first[sweep, pl.ds(step, 1)]
            flux_right = inner_face * (right_coef * (lasts - g) + nb_coef * (nb_first - g))
            gl = g_left[pl.ds(step, 1)]
            firsts = sent_first[sweep, pl.ds(step, 1)]
            nb_last = got_last[sweep, pl.ds(step, 1)]
            from_left = 1.0 * (nb_rcoef * (nb_last - gl) + left_coef * (firsts - gl))
            return jnp.where(has_left, from_left, 0.0), flux_right

        march_steps(waves, sigma, coil, coef.at[1], scaled_neu,
                    jnp.zeros((cols_n, subs, lanes), jnp.float32), False, neumann_terms,
                    keeper(trace_slot(sweep), neumann[0], sweep),
                    ends0 if sweep + 1 == SWEEPS else spare)
        send_rows(trace_slot(sweep), neumann[0], neumann[1], sweep, steps - 1)

    def last_update(step, carry):
        update_traces(SWEEPS - 1, step)
        return carry

    lax.fori_loop(0, steps, last_update, 0)


def relax(waveform, nu_table, packed):
    _, cols_n, subs, lanes = packed.shape
    steps = waveform.shape[0]
    vmem = pl.BlockSpec(memory_space=pltpu.VMEM)
    smem = pl.BlockSpec(memory_space=pltpu.SMEM)
    field = jax.ShapeDtypeStruct((cols_n, subs, lanes), jnp.float32)
    series = jax.ShapeDtypeStruct((steps, subs, lanes), jnp.float32)
    plane = pltpu.VMEM((steps, subs, lanes), jnp.float32)
    whole = pltpu.VMEM((cols_n, subs, lanes), jnp.float32)
    pair = pltpu.VMEM((SWEEPS, steps, subs, lanes), jnp.float32)
    two = pltpu.VMEM((2, subs, lanes), jnp.float32)
    return pl.pallas_call(
        relax_kernel,
        out_shape=(field, series),
        in_specs=[smem, smem, vmem],
        out_specs=(vmem, vmem),
        scratch_shapes=[
            pltpu.VMEM((10, cols_n, subs, lanes), jnp.float32),
            pair,
            pair,
            pair,
            pair,
            whole,
            whole,
            plane,
            two,
            two,
            pair,
            pair,
            pair,
            pair,
            whole,
            pltpu.SemaphoreType.DMA((3 + 8 * steps * SWEEPS,)),
            pltpu.SemaphoreType.DMA((3 + 8 * steps * SWEEPS,)),
        ],
        compiler_params=pltpu.CompilerParams(collective_id=0, has_side_effects=True),
    )(waveform, nu_table, packed)


def body(start_states, sigma, labels, nu_table, coil, waveform):
    states = start_states[0]
    cols_n, rows_n = states.shape
    packed = jnp.stack([states, sigma, coil, labels.astype(jnp.float32)])
    subs = rows_n // LANES
    packed = packed.reshape(4, cols_n, LANES, subs).transpose(0, 1, 3, 2)
    ends, traces = relax(waveform, nu_table, packed)
    ends = ends.transpose(0, 2, 1).reshape(1, cols_n, rows_n)
    traces = traces.transpose(0, 2, 1).reshape(traces.shape[0], rows_n)
    return (ends, traces)


def solution(mesh):
    placed = (
        P("tm", "space", None),
        P("space", None),
        P("space", None),
        P(),
        P("space", None),
        P("tm"),
    )
    return jax.shard_map(
        body,
        mesh=mesh,
        in_specs=placed,
        out_specs=(P("tm", "space", None), P("tm", "space")),
        check_vma=False,
    )
```

```python
import jax
import jax.numpy as jnp
from jax import lax
from jax.experimental import pallas as pl
from jax.experimental.pallas import tpu as pltpu
from jax.sharding import PartitionSpec as P

JACOBI = 8
SWEEPS = 2
LANES = 128


THETA = 0.25
MESH = pl.DeviceIdType.MESH


def harmonic(first_nu, second_nu):
    return 2.0 * first_nu * second_nu / (first_nu + second_nu)


def row_neighbours(field, at_first, at_last):
    subs, lanes = field.shape[1], field.shape[2]
    up = pltpu.roll(field, lanes - 1, 2)
    up = jnp.where(at_last, pltpu.roll(up, subs - 1, 1), up)
    down = pltpu.roll(field, 1, 2)
    down = jnp.where(at_first, pltpu.roll(down, 1, 1), down)
    return up, down


def march_steps(waves, sigma, coil, diag, scaled, start, forced, terms, after, end):
    cols_n, subs, lanes = start.shape
    lane = lax.broadcasted_iota(jnp.int32, (subs, lanes), 1)
    at_first = lane == 0
    at_last = lane == lanes - 1
    axp, axm, ayp, aym = scaled

    def advance(step, previous):
        rhs = sigma[...] * jnp.stack(previous)
        if forced:
            rhs = rhs + coil[...] * waves[step]
        left_val, right_val = terms(step)
        rhs = jnp.concatenate(
            [rhs[0:1] + left_val, rhs[1:cols_n - 1], rhs[cols_n - 1:] + right_val], axis=0
        )
        base = rhs / diag[...]
        field = list(previous)
        for repeat in range(JACOBI):
            fresh = []
            for col in range(cols_n):
                here = field[col]
                up = pltpu.roll(here, lanes - 1, 1)
                up = jnp.where(at_last, pltpu.roll(up, subs - 1, 0), up)
                down = pltpu.roll(here, 1, 1)
                down = jnp.where(at_first, pltpu.roll(down, 1, 0), down)
                across = base[col]
                if col + 1 < cols_n:
                    across = across + axp[col] * field[col + 1]
                if col > 0:
                    across = across + axm[col] * field[col - 1]
                fresh.append(across + (ayp[col] * up + aym[col] * down))
            field = fresh
        after(step, field)
        return tuple(field)

    done = lax.fori_loop(0, waves.shape[0], advance,
                         tuple(start[col] for col in range(cols_n)))
    end[...] = jnp.stack(done)


def relax_kernel(waves, table, packed, out_ends, out_traces,
                 coef, sent_first, sent_last, pfirst, plast, ends0, spare, g_left,
                 own_coefs, got_coefs, got_first, got_last, got_pfirst, got_plast, got_state, ends, traces,
                 send_sem, recv_sem):
    _, cols_n, subs, lanes = packed.shape
    steps = traces.shape[0]
    n_space = lax.axis_size("space")
    n_tm = lax.axis_size("tm")
    me_s = lax.axis_index("space")
    me_t = lax.axis_index("tm")
    has_left = me_s > 0
    has_right = me_s < n_space - 1
    no_left = jnp.logical_not(has_left)
    no_right = jnp.logical_not(has_right)
    left = (me_t, lax.rem(me_s + n_space - 1, n_space))
    right = (me_t, lax.rem(me_s + 1, n_space))
    tm_next = (lax.rem(me_t + 1, n_tm), me_s)
    tm_prev = (lax.rem(me_t + n_tm - 1, n_tm), me_s)

    @pl.when(no_right)
    def _():
        got_first[...] = jnp.zeros(got_first.shape, jnp.float32)
        got_pfirst[...] = jnp.zeros(got_pfirst.shape, jnp.float32)
        got_coefs[0] = jnp.zeros(got_coefs.shape[1:], jnp.float32)

    @pl.when(no_left)
    def _():
        got_last[...] = jnp.zeros(got_last.shape, jnp.float32)
        got_plast[...] = jnp.zeros(got_plast.shape, jnp.float32)
        got_coefs[1] = jnp.zeros(got_coefs.shape[1:], jnp.float32)

    barrier = pltpu.get_barrier_semaphore()

    @pl.when(has_left)
    def _():
        pl.semaphore_signal(barrier, inc=1, device_id=left, device_id_type=MESH)

    @pl.when(has_right)
    def _():
        pl.semaphore_signal(barrier, inc=1, device_id=right, device_id_type=MESH)

    pl.semaphore_signal(barrier, inc=1, device_id=tm_next, device_id_type=MESH)
    pl.semaphore_signal(barrier, inc=1, device_id=tm_prev, device_id_type=MESH)
    pl.semaphore_wait(barrier, 2 + has_left.astype(jnp.int32) + has_right.astype(jnp.int32))

    def copy_of(slot, src, dst, target):
        return pltpu.make_async_remote_copy(
            src_ref=src, dst_ref=dst, send_sem=send_sem.at[slot],
            recv_sem=recv_sem.at[slot], device_id=target, device_id_type=MESH,
        )

    def start_if(copy, sends):
        @pl.when(sends)
        def _():
            copy.start()

    def wait_send_if(copy, sends):
        @pl.when(sends)
        def _():
            copy.wait_send()

    def wait_recv_if(copy, receives):
        @pl.when(receives)
        def _():
            copy.wait_recv()

    sigma = packed.at[1]
    coil = packed.at[2]
    labels = packed[3]
    nu = jnp.zeros(labels.shape, jnp.float32)
    for material in range(table.shape[0]):
        nu = nu + jnp.where(labels == jnp.float32(material), table[material], jnp.float32(0.0))
    left_coef = 2.0 * nu[0:1]
    right_coef = 2.0 * nu[cols_n - 1:]
    own_coefs[0] = left_coef[0]
    own_coefs[1] = right_coef[0]
    coef_left = copy_of(0, own_coefs.at[0], got_coefs.at[0], left)
    coef_right = copy_of(1, own_coefs.at[1], got_coefs.at[1], right)
    start_if(coef_left, has_left)
    start_if(coef_right, has_right)

    lane = lax.broadcasted_iota(jnp.int32, (1, subs, lanes), 2)
    row = lax.broadcasted_iota(jnp.int32, (1, subs, lanes), 1) * lanes + lane
    rows_n = subs * lanes
    up, down = row_neighbours(nu, lane == 0, lane == lanes - 1)
    up = jnp.where(row == rows_n - 1, 0.0, up)
    down = jnp.where(row == 0, 0.0, down)
    blank = jnp.zeros((1, subs, lanes), jnp.float32)
    east = jnp.concatenate([nu[1:], blank], axis=0)
    west = jnp.concatenate([blank, nu[:cols_n - 1]], axis=0)
    kxp = harmonic(nu, east)
    kxm = harmonic(nu, west)
    kyp = harmonic(nu, up)
    kym = harmonic(nu, down)
    edge_rows = jnp.where((row == 0) | (row == rows_n - 1), 1.0, 0.0).astype(jnp.float32)
    inner = sigma[...] + kxp + kxm + kyp + kym + 2.0 * nu * edge_rows
    first_f = jnp.where(has_left, 0.0, 1.0).astype(jnp.float32)
    last_f = jnp.where(has_right, 0.0, 1.0).astype(jnp.float32)
    inner_face = 1.0 - last_f
    d_dir = jnp.concatenate(
        [inner[0:1] + left_coef, inner[1:cols_n - 1], inner[cols_n - 1:] + right_coef], axis=0
    )
    d_neu = jnp.concatenate(
        [inner[0:1] + first_f * left_coef, inner[1:cols_n - 1],
         inner[cols_n - 1:] + last_f * right_coef], axis=0
    )
    coef[0] = d_dir
    coef[1] = d_neu
    for index, k in enumerate((kxp, kxm, kyp, kym)):
        coef[2 + index] = k / d_dir
        coef[6 + index] = k / d_neu
    scaled_dir = tuple(coef.at[2 + index] for index in range(4))
    scaled_neu = tuple(coef.at[6 + index] for index in range(4))

    wait_send_if(coef_left, has_left)
    wait_send_if(coef_right, has_right)
    wait_recv_if(coef_left, has_right)
    wait_recv_if(coef_right, has_left)
    nb_coef = got_coefs[0][None]
    nb_rcoef = got_coefs[1][None]

    def row_copies(slot, src, dst, sweep, step):
        to_left = copy_of(slot + step, src[0].at[sweep, pl.ds(step, 1)],
                          dst[0].at[sweep, pl.ds(step, 1)], left)
        to_right = copy_of(slot + steps + step, src[1].at[sweep, pl.ds(step, 1)],
                           dst[1].at[sweep, pl.ds(step, 1)], right)
        return to_left, to_right

    def send_rows(slot, src, dst, sweep, step):
        to_left, to_right = row_copies(slot, src, dst, sweep, step)
        start_if(to_left, has_left)
        start_if(to_right, has_right)

    def settle_rows(slot, src, dst, sweep, step):
        to_left, to_right = row_copies(slot, src, dst, sweep, step)
        wait_send_if(to_left, has_left)
        wait_send_if(to_right, has_right)
        wait_recv_if(to_left, has_right)
        wait_recv_if(to_right, has_left)

    def face_slot(sweep):
        return 3 + 8 * steps * sweep

    def trace_slot(sweep):
        return 3 + 8 * steps * sweep + 4 * steps

    faces = ((sent_first, sent_last), (got_first, got_last))
    neumann = ((pfirst, plast), (got_pfirst, got_plast))

    def update_traces(sweep, step):
        settle_rows(trace_slot(sweep), neumann[0], neumann[1], sweep, step)
        g = traces[pl.ds(step, 1)]
        g = g + THETA * inner_face * (plast[sweep, pl.ds(step, 1)] + got_pfirst[sweep, pl.ds(step, 1)])
        traces[pl.ds(step, 1)] = g
        gl = g_left[pl.ds(step, 1)]
        gl = gl + THETA * 1.0 * (got_plast[sweep, pl.ds(step, 1)] + pfirst[sweep, pl.ds(step, 1)])
        gl = jnp.where(has_left, gl, 0.0)
        g_left[pl.ds(step, 1)] = gl
        return g, gl

    def keeper(slot, rows, sweep):
        def after(step, field):
            rows[0][sweep, pl.ds(step, 1)] = field[0][None]
            rows[1][sweep, pl.ds(step, 1)] = field[cols_n - 1][None]

            @pl.when(step > 0)
            def _():
                send_rows(slot, rows, faces[1] if rows is faces[0] else neumann[1],
                          sweep, step - 1)

        return after

    traces[...] = jnp.zeros(traces.shape, jnp.float32)
    g_left[...] = jnp.zeros(g_left.shape, jnp.float32)
    start = packed[0]
    state_copy = copy_of(2, ends0, got_state, tm_next)
    for sweep in range(SWEEPS):
        if sweep > 0:
            state_copy.wait_send()
            state_copy.wait_recv()
            start = got_state[...]

            def dirichlet_terms(step, sweep=sweep):
                g, gl = update_traces(sweep - 1, step)
                return left_coef * gl, right_coef * g
        else:
            def dirichlet_terms(step):
                return blank, blank
        end = ends if sweep + 1 == SWEEPS else ends0
        march_steps(waves, sigma, coil, coef.at[0], scaled_dir, start, True, dirichlet_terms,
                    keeper(face_slot(sweep), faces[0], sweep), end)
        send_rows(face_slot(sweep), faces[0], faces[1], sweep, steps - 1)
        if sweep + 1 < SWEEPS:
            state_copy.start()

        def neumann_terms(step, sweep=sweep):
            settle_rows(face_slot(sweep), faces[0], faces[1], sweep, step)
            g = traces[pl.ds(step, 1)]
            lasts = sent_last[sweep, pl.ds(step, 1)]
            nb_first = got_first[sweep, pl.ds(step, 1)]
            flux_right = inner_face * (right_coef * (lasts - g) + nb_coef * (nb_first - g))
            gl = g_left[pl.ds(step, 1)]
            firsts = sent_first[sweep, pl.ds(step, 1)]
            nb_last = got_last[sweep, pl.ds(step, 1)]
            from_left = 1.0 * (nb_rcoef * (nb_last - gl) + left_coef * (firsts - gl))
            return jnp.where(has_left, from_left, 0.0), flux_right

        march_steps(waves, sigma, coil, coef.at[1], scaled_neu,
                    jnp.zeros((cols_n, subs, lanes), jnp.float32), False, neumann_terms,
                    keeper(trace_slot(sweep), neumann[0], sweep),
                    ends0 if sweep + 1 == SWEEPS else spare)
        send_rows(trace_slot(sweep), neumann[0], neumann[1], sweep, steps - 1)

    def last_update(step, carry):
        update_traces(SWEEPS - 1, step)
        return carry

    lax.fori_loop(0, steps, last_update, 0)
    for src, dst in ((ends, out_ends), (traces, out_traces)):
        for item in range(src.shape[0]):
            block = src[item]
            for part in range(subs):
                dst[pl.ds(item, 1), pl.ds(part * lanes, lanes)] = block[part:part + 1]


def relax(waveform, nu_table, packed):
    _, cols_n, subs, lanes = packed.shape
    steps = waveform.shape[0]
    vmem = pl.BlockSpec(memory_space=pltpu.VMEM)
    smem = pl.BlockSpec(memory_space=pltpu.SMEM)
    field = jax.ShapeDtypeStruct((cols_n, subs * lanes), jnp.float32)
    series = jax.ShapeDtypeStruct((steps, subs * lanes), jnp.float32)
    plane = pltpu.VMEM((steps, subs, lanes), jnp.float32)
    whole = pltpu.VMEM((cols_n, subs, lanes), jnp.float32)
    pair = pltpu.VMEM((SWEEPS, steps, subs, lanes), jnp.float32)
    two = pltpu.VMEM((2, subs, lanes), jnp.float32)
    return pl.pallas_call(
        relax_kernel,
        out_shape=(field, series),
        in_specs=[smem, smem, vmem],
        out_specs=(vmem, vmem),
        scratch_shapes=[
            pltpu.VMEM((10, cols_n, subs, lanes), jnp.float32),
            pair,
            pair,
            pair,
            pair,
            whole,
            whole,
            plane,
            two,
            two,
            pair,
            pair,
            pair,
            pair,
            whole,
            whole,
            plane,
            pltpu.SemaphoreType.DMA((3 + 8 * steps * SWEEPS,)),
            pltpu.SemaphoreType.DMA((3 + 8 * steps * SWEEPS,)),
        ],
        compiler_params=pltpu.CompilerParams(collective_id=0, has_side_effects=True),
    )(waveform, nu_table, packed)


def body(start_states, sigma, labels, nu_table, coil, waveform):
    states = start_states[0]
    cols_n, rows_n = states.shape
    packed = jnp.stack([states, sigma, coil, labels.astype(jnp.float32)])
    packed = packed.reshape(4, cols_n, rows_n // LANES, LANES)
    ends, traces = relax(waveform, nu_table, packed)
    return (ends[None], traces)


def solution(mesh):
    placed = (
        P("tm", "space", None),
        P("space", None),
        P("space", None),
        P(),
        P("space", None),
        P("tm"),
    )
    return jax.shard_map(
        body,
        mesh=mesh,
        in_specs=placed,
        out_specs=(P("tm", "space", None), P("tm", "space")),
        check_vma=False,
    )
```
